512 devices in a mesh: row: 16 (over x, z_lo), col: 32 (over y, z_hi, core).
Axes of the slice: x: 4, y: 4, z: 16 (z_hi: 4, z_lo: 4; z = z_hi * 4 + z_lo), core: 2. Of those that a mesh axis runs over, the one named last changes fastest.
Arguments:
- features: bfloat16 [65536, 256], P(('col', 'row')), may hold values from -6 to 6
- weight: bfloat16 [256, 256], replicated, may hold values from -0.375 to 0.375
- cotangent: bfloat16 [65536, 256], P(('row', 'col')), may hold values from -6 to 6
- block_index: int32 [16, 32, 32], P('row', 'col'), may hold values from 0 to 511, as said below
- block_count: int32 [16, 32], P('row', 'col'), may hold values from 1 to 32, as said below
- block_values: bfloat16 [16, 32, 32, 128, 128], P('row', 'col'), may hold values from -0.125 to 0.125
Outputs:
- hidden_out: bfloat16 [65536, 256], P(('row', 'col'))
- input_grad: bfloat16 [65536, 256], P(('col', 'row'))
- weight_grad: float32 [256, 256], replicated
The draws below stay inside these ranges and needn't reach their ends.
Inputs may be any that keep to these rules, and one draw needn't show every extreme that they name: `block_index`: the 32 entries of one tile are distinct; slots at or after the tile's count hold blocks that are not used. `block_count`: at least one tile holds exactly 32 blocks.
All inputs are finite; a program needn't handle non-finite values.
Results may differ from the reference program's by a relative error of at most 0.015.
Values may be sent and summed in bfloat16 or wider, within the bound.
A program may use at most 64 MiB of HBM per device.

```python
import math
import jax
import jax.numpy as jnp
from jax import lax

D = 256
BS = 128
GROUP = 32
BR = 32
MAXB = 32
BC = 16
NODES = 65536
FANIN = 2048
N_ROW = 16
N_COL = 32


def draw_block_index(key, part):
    keys = jax.random.split(jax.random.fold_in(key, 11), N_ROW * N_COL)

    def one_tile(tile_key):
        return jax.random.permutation(tile_key, BR * BC)[:MAXB].astype(jnp.int32)
    return jax.vmap(one_tile)(keys).reshape(N_ROW, N_COL, MAXB)


def draw_block_count(key, part):
    base = jax.random.fold_in(key, 23)
    first_key, second_key, third_key = jax.random.split(base, 3)
    first = jax.random.randint(first_key, (N_ROW * N_COL,), 0, 17)
    second = jax.random.randint(second_key, (N_ROW * N_COL,), 0, 17)
    counts = MAXB // 4 + (MAXB - MAXB // 4) * first * second // 256
    counts = jnp.maximum(counts, 1)
    chosen = jax.random.randint(third_key, (), 0, N_ROW * N_COL)
    counts = counts.at[chosen].set(MAXB)
    return counts.astype(jnp.int32).reshape(N_ROW, N_COL)


def steps_of(key, extent, shards, low, top_value):
    def one(axis_at, shards_of):
        steps = jax.random.uniform(jax.random.fold_in(jax.random.fold_in(key, 6), axis_at), (shards_of,), jnp.float32, low / len(shards), top_value / len(shards))
        return jnp.repeat(jnp.exp(steps), extent[axis_at] // shards_of).reshape((-1,) + (1,) * (len(extent) - axis_at - 1))

    level = one(*shards[0])
    for cut in shards[1:]:
        level = level * one(*cut)
    return level


def noise(stream_key, shape, scale, most, cuts=(), held_as=jnp.bfloat16):
    result = scale * jax.random.normal(stream_key, shape, jnp.float32)
    if cuts:
        result = result * steps_of(stream_key, shape, cuts, -0.22, 0.18)
    return jnp.clip(result, -most, most).astype(held_as)


def setup_inputs(seed: int = 0) -> dict:
    key_list = jax.random.split(jax.random.key(seed), 7)
    return {
        "features": noise(key_list[0], (NODES, D), 1.0, 6.0, ((0, 512),)),
        "weight": noise(key_list[1], (D, D), D ** -0.5, 0.375),
        "cotangent": noise(key_list[2], (NODES, D), 1.0, 6.0, ((0, 512),)),
        "block_index": draw_block_index(jax.random.fold_in(key_list[6], 71), 0),
        "block_count": draw_block_count(jax.random.fold_in(key_list[6], 71), 0),
        "block_values": noise(key_list[5], (N_ROW, N_COL, MAXB, BS, BS), FANIN ** -0.5, 0.125, ((0, 16), (1, 32))),
    }


def forward_tile(blocks_in, values, index, count, rows_out):
    ncols = blocks_in.shape[0]
    size = blocks_in.shape[1]
    width = blocks_in.shape[2]
    lanes = jnp.arange(GROUP, dtype=jnp.int32)
    targets = jnp.arange(rows_out, dtype=jnp.int32)

    def advance(group_id, totals):
        start = (group_id * GROUP).astype(jnp.int32)
        group_values = lax.dynamic_slice_in_dim(values, start, GROUP, 0)
        group_ids = lax.dynamic_slice_in_dim(index, start, GROUP, 0).astype(jnp.int32)
        live = start + lanes < count
        picked = jnp.take(blocks_in, group_ids % ncols, axis=0)
        product = jnp.einsum('gij,gjd->gid', group_values.astype(jnp.float32), picked.astype(jnp.float32), precision=lax.Precision.HIGHEST)
        selector = ((group_ids // ncols)[None, :] == targets[:, None]) & live[None, :]
        return totals + jnp.einsum('rg,gid->rid', selector.astype(jnp.float32), product, precision=lax.Precision.HIGHEST)
    zeros = jnp.zeros((rows_out, size, width), jnp.float32)
    groups = ((count + GROUP - 1) // GROUP).astype(jnp.int32)
    return lax.fori_loop(jnp.int32(0), groups, advance, zeros)

def backward_tile(blocks_grad, values, index, count, cols_out):
    size = blocks_grad.shape[1]
    width = blocks_grad.shape[2]
    lanes = jnp.arange(GROUP, dtype=jnp.int32)
    targets = jnp.arange(cols_out, dtype=jnp.int32)

    def advance(group_id, totals):
        start = (group_id * GROUP).astype(jnp.int32)
        group_values = lax.dynamic_slice_in_dim(values, start, GROUP, 0)
        group_ids = lax.dynamic_slice_in_dim(index, start, GROUP, 0).astype(jnp.int32)
        live = start + lanes < count
        picked = jnp.take(blocks_grad, group_ids // cols_out, axis=0)
        product = jnp.einsum('gij,gid->gjd', group_values.astype(jnp.float32), picked.astype(jnp.float32), precision=lax.Precision.HIGHEST)
        selector = ((group_ids % cols_out)[None, :] == targets[:, None]) & live[None, :]
        return totals + jnp.einsum('cg,gjd->cjd', selector.astype(jnp.float32), product, precision=lax.Precision.HIGHEST)
    zeros = jnp.zeros((cols_out, size, width), jnp.float32)
    groups = ((count + GROUP - 1) // GROUP).astype(jnp.int32)
    return lax.fori_loop(jnp.int32(0), groups, advance, zeros)

def reference(features, weight, cotangent, block_index, block_count, block_values):
    projected = jnp.dot(features, weight, preferred_element_type=jnp.float32).astype(jnp.bfloat16)
    total_blocks = BR * N_ROW
    proj_blocks = projected.reshape(total_blocks, BS, D)
    grad_blocks = cotangent.reshape(total_blocks, BS, D)
    tiles = N_ROW * N_COL
    flat_index = block_index.reshape(tiles, MAXB)
    flat_count = block_count.reshape(tiles)
    flat_values = block_values.reshape(tiles, MAXB, BS, BS)

    def visit(tile, carry):
        out_acc, back_acc = carry
        tile = tile.astype(jnp.int32)
        row_start = (tile // N_COL * BR).astype(jnp.int32)
        col_start = (tile % N_COL * BC).astype(jnp.int32)
        values = lax.dynamic_index_in_dim(flat_values, tile, 0, keepdims=False)
        index = lax.dynamic_index_in_dim(flat_index, tile, 0, keepdims=False)
        count = lax.dynamic_index_in_dim(flat_count, tile, 0, keepdims=False)
        inputs = lax.dynamic_slice_in_dim(proj_blocks, col_start, BC, 0)
        part = forward_tile(inputs, values, index, count, BR)
        rounded = lax.optimization_barrier(part.astype(jnp.bfloat16)).astype(jnp.float32)
        current = lax.dynamic_slice_in_dim(out_acc, row_start, BR, 0)
        out_acc = lax.dynamic_update_slice_in_dim(out_acc, current + rounded, row_start, 0)
        grads = lax.dynamic_slice_in_dim(grad_blocks, row_start, BR, 0)
        back = backward_tile(grads, values, index, count, BC)
        back_rounded = lax.optimization_barrier(back.astype(jnp.bfloat16)).astype(jnp.float32)
        current_back = lax.dynamic_slice_in_dim(back_acc, col_start, BC, 0)
        back_acc = lax.dynamic_update_slice_in_dim(back_acc, current_back + back_rounded, col_start, 0)
        return (out_acc, back_acc)
    zeros = jnp.zeros((total_blocks, BS, D), jnp.float32)
    out_acc, back_acc = lax.fori_loop(jnp.int32(0), jnp.int32(tiles), visit, (zeros, zeros))
    hidden_out = out_acc.reshape(NODES, D).astype(jnp.bfloat16)
    grad_sum = back_acc.reshape(NODES, D)
    input_grad = jnp.dot(grad_sum, weight.astype(jnp.float32).T, precision=lax.Precision.HIGHEST).astype(jnp.bfloat16)
    weight_grad = jnp.dot(features.astype(jnp.float32).T, grad_sum, precision=lax.Precision.HIGHEST) / math.sqrt(NODES)
    return (hidden_out, input_grad, weight_grad)
```

```python
import functools
import math

import jax
import jax.numpy as jnp
from jax import lax
from jax.experimental import pallas as pl
from jax.experimental.pallas import tpu as pltpu
from jax.sharding import PartitionSpec as P

MESH = pl.DeviceIdType.MESH
BF = jnp.bfloat16
F32 = jnp.float32
RING = 4
ORDER = (2, 1, 3, 0)


def ids():
    table = {}

    def of(*key):
        return table.setdefault(key, len(table))

    return of


COPIES = 128


def kernel(
    feat, weight, cot, idxv, idxs, cnt, vals,
    out_o, ig_o, wg_o,
    fa, ca, proj, run, pout, pback, tbl_v, tbl_s,
    rc, sy, own_y, ry, sz, rz, rx, szl, rzl,
    wacc, w1s, w1r, w1, w2s, w2r, w2, w3r, w4, w5,
    ss, rs, ls,
):
    of = ids()
    row = lax.axis_index("row")
    col = lax.axis_index("col")
    x, zl = row // 4, lax.rem(row, 4)
    y, zh, c = col // 8, lax.rem(col // 2, 4), lax.rem(col, 2)
    sib = 1 - c

    def r4(v):
        return lax.rem(v, 4)

    def dev(x_=x, zl_=zl, y_=y, zh_=zh, c_=c):
        return (x_ * 4 + zl_, y_ * 8 + zh_ * 2 + c_)

    def at(axis, k):
        here = {"x": x, "zl": zl, "y": y, "zh": zh}[axis]
        there = r4(here + k)
        return dev(**{axis + "_": there}), there

    sends = []

    def send(src, dst, key, device):
        n = of(*key)
        copy = pltpu.make_async_remote_copy(
            src_ref=src, dst_ref=dst, send_sem=ss.at[n], recv_sem=rs.at[n],
            device_id=device, device_id_type=MESH,
        )
        copy.start()
        sends.append(copy)

    def arrive(dst, key):
        n = of(*key)
        pltpu.make_async_remote_copy(
            src_ref=dst, dst_ref=dst, send_sem=ss.at[n], recv_sem=rs.at[n],
            device_id=dev(c_=sib), device_id_type=MESH,
        ).wait_recv()

    barrier = pltpu.get_barrier_semaphore()
    partners = [at(a, k)[0] for a in ("x", "zl", "y", "zh") for k in (1, 2, 3)]
    partners.append(dev(c_=sib))
    for p in partners:
        pl.semaphore_signal(barrier, inc=1, device_id=p, device_id_type=MESH)

    fa[row] = feat[...]
    ca[col] = cot[...]

    lane = lax.broadcasted_iota(jnp.int32, (1, 128), 1)
    tbl_v[...] = jnp.zeros_like(tbl_v)
    tbl_v[0:1, 0:32] = idxv[...]
    index = tbl_v[0:1, :]
    srow, scol = index // 16, lax.rem(index, jnp.full_like(index, 16))
    count = cnt[0, 0]
    none = jnp.full((1, 128), 32, jnp.int32)

    def link(t, carry):
        pf, lf, pb, lb = carry
        i = idxs[0, t]
        ti, tj = i // 16, lax.rem(i, 16)
        later = lane > t
        pf = jnp.where(later & (srow == ti), t, pf)
        pb = jnp.where(later & (scol == tj), t, pb)
        live = jnp.full((1, 128), t, jnp.int32) < count
        lf = jnp.where(live & (lane == ti), t, lf)
        lb = jnp.where(live & (lane == tj), t, lb)
        return pf, lf, pb, lb

    pf, lf, pb, lb = lax.fori_loop(0, 32, link, (none, none, none, none))
    tbl_v[0:1, :] = scol
    tbl_v[1:2, :] = pf
    tbl_v[2:3, :] = lf
    tbl_v[3:4, :] = srow
    tbl_v[4:5, :] = pb
    tbl_v[5:6, :] = lb
    table = pltpu.make_async_copy(tbl_v, tbl_s, ls)
    table.start()

    pl.semaphore_wait(barrier, len(partners))

    def features_on(block, tag):
        for k in (1, 2, 3):
            d, _ = at("x", k)
            send(fa.at[block], fa.at[block], ("fx", k, tag), d)

    def cotangents_on(block, tag):
        for k in (1, 2, 3):
            d, _ = at("y", k)
            send(ca.at[block], ca.at[block], ("cy", k, tag), d)
        send(ca.at[block], ca.at[block], ("cs", 0, tag), dev(c_=sib))

    for k in (1, 3, 2):
        send(fa.at[row], fa.at[row], ("fz", k), at("zl", k)[0])
    for k in (1, 3, 2):
        send(ca.at[col], ca.at[col], ("cz", k), at("zh", k)[0])
    features_on(row, 0)
    cotangents_on(col, 0)
    for k in (1, 3, 2):
        block = x * 4 + r4(zl + 4 - k)
        arrive(fa.at[block], ("fz", k))
        features_on(block, k)
    for k in (1, 3, 2):
        block = y * 8 + r4(zh + 4 - k) * 2 + c
        arrive(ca.at[block], ("cz", k))
        cotangents_on(block, k)

    table.wait()
    run[32] = jnp.zeros_like(run[32])

    for tag in (0, 1, 3, 2):
        for k in (1, 3, 2):
            block = r4(x + 4 - k) * 4 + r4(zl + 4 - tag)
            arrive(fa.at[block], ("fx", k, tag))

    def project(j, carry):
        proj[j] = jnp.dot(fa[j], weight[...], preferred_element_type=F32).astype(BF)
        return carry

    lax.fori_loop(0, 16, project, 0)

    def forward(s, carry):
        product = jnp.dot(vals[s], proj[tbl_s[0, s]], preferred_element_type=F32)
        run[s] = product + run[tbl_s[1, s]]
        return carry

    lax.fori_loop(0, 32, forward, 0)

    def forward_out(o, carry):
        r = lax.rem(o, 4) * 8 + lax.rem(o // 4, 4) * 2 + o // 16
        pout[o] = run[tbl_s[2, r]].astype(BF)
        return carry

    lax.fori_loop(0, 32, forward_out, 0)

    def group(g):
        return r4(zh + ORDER[g])

    for g in range(4):
        part = pl.ds(sib * 16 + group(g) * 4, 4)
        send(pout.at[part], rc.at[pl.ds(g * 4, 4)], ("oc", g), dev(c_=sib))

    for tag in (0, 1, 3, 2):
        for k in (1, 3, 2):
            block = r4(y + 4 - k) * 8 + r4(zh + 4 - tag) * 2 + c
            arrive(ca.at[block], ("cy", k, tag))
            send(ca.at[block], ca.at[block], ("cs", k, tag), dev(c_=sib))

    for g in range(4):
        arrive(rc.at[pl.ds(g * 4, 4)], ("oc", g))
        for k in (2, 1, 3):
            d, there = at("y", k)
            own = pout[c * 16 + group(g) * 4 + there].astype(F32)
            sy[g * 3 + k - 1] = (own + rc[g * 4 + there].astype(F32)).astype(BF)
            send(sy.at[g * 3 + k - 1], ry.at[g * 3 + k - 1], ("oy", g, k), d)
        own_y[g] = pout[c * 16 + group(g) * 4 + y].astype(F32) + rc[g * 4 + y].astype(F32)

    for tag in (0, 1, 3, 2):
        for k in (0, 1, 3, 2):
            block = r4(y + 4 - k) * 8 + r4(zh + 4 - tag) * 2 + sib
            arrive(ca.at[block], ("cs", k, tag))

    def backward(s, carry):
        product = lax.dot_general(
            vals[s], ca[tbl_s[3, s]], (((0,), (0,)), ((), ())), preferred_element_type=F32
        )
        run[s] = product + run[tbl_s[4, s]]
        return carry

    lax.fori_loop(0, 32, backward, 0)

    def backward_out(j, carry):
        pback[j] = run[tbl_s[5, j]].astype(BF)
        return carry

    lax.fori_loop(0, 16, backward_out, 0)

    for g in range(4):
        zt = r4(zl + ORDER[g])
        for k in (2, 1, 3):
            d, there = at("x", k)
            send(pback.at[there * 4 + zt], rx.at[g * 3 + k - 1], ("bx", g, k), d)

    wacc[...] = jnp.zeros_like(wacc)

    def weight_term(j, carry):
        wacc[...] += lax.dot_general(
            fa[j], pback[j], (((0,), (0,)), ((), ())), preferred_element_type=F32
        )
        return carry

    lax.fori_loop(0, 16, weight_term, 0)
    w1s[...] = wacc[pl.ds(pl.multiple_of(sib * 128, 128), 128), :].astype(BF)
    send(w1s, w1r, ("w1",), dev(c_=sib))

    def total_y(g):
        total = own_y[g]
        for k in (1, 2, 3):
            arrive(ry.at[g * 3 + k - 1], ("oy", g, k))
            total = total + ry[g * 3 + k - 1].astype(F32)
        return total

    for g in range(3):
        sz[g] = total_y(g).astype(BF)
        send(sz.at[g], rz.at[g], ("oz", g), at("zh", ORDER[g])[0])

    arrive(w1r, ("w1",))
    w1[...] = wacc[pl.ds(pl.multiple_of(c * 128, 128), 128), :] + w1r[...].astype(F32)
    for k in (2, 1, 3):
        d, there = at("x", k)
        w2s[k - 1] = w1[pl.ds(pl.multiple_of(there * 32, 32), 32), :].astype(BF)
        send(w2s.at[k - 1], w2r.at[k - 1], ("w2", k), d)

    def total_x(g):
        total = pback[x * 4 + r4(zl + ORDER[g])].astype(F32)
        for k in (1, 2, 3):
            arrive(rx.at[g * 3 + k - 1], ("bx", g, k))
            total = total + rx[g * 3 + k - 1].astype(F32)
        return total

    for g in range(3):
        szl[g] = total_x(g).astype(BF)
        send(szl.at[g], rzl.at[g], ("bz", g), at("zl", ORDER[g])[0])

    piece = w1[pl.ds(pl.multiple_of(x * 32, 32), 32), :]
    for k in (1, 2, 3):
        arrive(w2r.at[k - 1], ("w2", k))
        piece = piece + w2r[k - 1].astype(F32)
    w2[...] = piece.reshape(4, 8, 256)
    for k in (2, 1, 3):
        d, there = at("y", k)
        send(w2.at[there], w3r.at[k - 1], ("w3", k), d)

    total = total_y(3)
    for g in range(3):
        arrive(rz.at[g], ("oz", g))
        total = total + rz[g].astype(F32)
    out_o[...] = total.astype(BF)

    small = w2[y]
    for k in (1, 2, 3):
        arrive(w3r.at[k - 1], ("w3", k))
        small = small + w3r[k - 1]
    w4[zl] = small
    for k in (2, 1, 3):
        send(w4.at[zl], w4.at[zl], ("w4", k), at("zl", k)[0])

    grad = total_x(3)
    for g in range(3):
        arrive(rzl.at[g], ("bz", g))
        grad = grad + rzl[g].astype(F32)
    high = grad.astype(BF)
    low = (grad - high.astype(F32)).astype(BF)
    nt = (((1,), (1,)), ((), ()))
    ig_o[...] = (
        lax.dot_general(high, weight[...], nt, preferred_element_type=F32)
        + lax.dot_general(low, weight[...], nt, preferred_element_type=F32)
    ).astype(BF)

    for k in (1, 2, 3):
        arrive(w4.at[r4(zl + 4 - k)], ("w4", k))
    w5[zh] = ((w4[0] + w4[1]) + w4[2]) + w4[3]
    for k in (2, 1, 3):
        send(w5.at[zh], w5.at[zh], ("w5", k), at("zh", k)[0])
    for k in (1, 2, 3):
        arrive(w5.at[r4(zh + 4 - k)], ("w5", k))
    scale = 1.0 / math.sqrt(65536)

    def rows_of(c_, x_, y_):
        return pl.multiple_of(c_ * 128 + x_ * 32 + y_ * 8, 8)

    mine = wg_o.at[pl.ds(rows_of(c, x, y), 8)]
    mine[...] = (((w5[0] + w5[1]) + w5[2]) + w5[3]) * scale
    for k in (2, 1, 3):
        send(mine, mine, ("w6", k), at("y", k)[0])
    for k in (1, 2, 3):
        arrive(wg_o.at[pl.ds(rows_of(c, x, r4(y + 4 - k)), 8)], ("w6", k))
    mine = wg_o.at[pl.ds(rows_of(c, x, 0), 32)]
    for k in (2, 1, 3):
        send(mine, mine, ("w7", k), at("x", k)[0])
    for k in (1, 2, 3):
        arrive(wg_o.at[pl.ds(rows_of(c, r4(x + 4 - k), 0), 32)], ("w7", k))
    mine = wg_o.at[pl.ds(rows_of(c, 0, 0), 128)]
    send(mine, mine, ("w8",), dev(c_=sib))
    arrive(wg_o.at[pl.ds(rows_of(sib, 0, 0), 128)], ("w8",))

    for copy in sends:
        copy.wait_send()


def body(features, weight, cotangent, block_index, block_count, block_values):
    vmem = pl.BlockSpec(memory_space=pltpu.VMEM)
    smem = pl.BlockSpec(memory_space=pltpu.SMEM)
    index = block_index.reshape(1, 32)
    blocks = functools.partial(lambda dtype, n: pltpu.VMEM((n, 128, 256), dtype))
    return pl.pallas_call(
        kernel,
        out_shape=(
            jax.ShapeDtypeStruct((128, 256), BF),
            jax.ShapeDtypeStruct((128, 256), BF),
            jax.ShapeDtypeStruct((256, 256), F32),
        ),
        in_specs=[vmem, vmem, vmem, vmem, smem, smem, vmem],
        out_specs=(vmem, vmem, vmem),
        scratch_shapes=[
            blocks(BF, 16), blocks(BF, 32), blocks(BF, 16), blocks(F32, 33),
            blocks(BF, 32), blocks(BF, 16),
            pltpu.VMEM((8, 128), jnp.int32), pltpu.SMEM((8, 128), jnp.int32),
            blocks(BF, 16), blocks(BF, 12), blocks(F32, 4), blocks(BF, 12),
            blocks(BF, 3), blocks(BF, 3), blocks(BF, 12), blocks(BF, 3), blocks(BF, 3),
            pltpu.VMEM((256, 256), F32), pltpu.VMEM((128, 256), BF), pltpu.VMEM((128, 256), BF),
            pltpu.VMEM((128, 256), F32), pltpu.VMEM((3, 32, 256), BF), pltpu.VMEM((3, 32, 256), BF),
            pltpu.VMEM((4, 8, 256), F32), pltpu.VMEM((3, 8, 256), F32),
            pltpu.VMEM((4, 8, 256), F32), pltpu.VMEM((4, 8, 256), F32),
            pltpu.SemaphoreType.DMA((COPIES,)), pltpu.SemaphoreType.DMA((COPIES,)),
            pltpu.SemaphoreType.DMA,
        ],
        compiler_params=pltpu.CompilerParams(
            collective_id=0, has_side_effects=True, vmem_limit_bytes=48 << 20
        ),
        name="graph_step",
    )(features, weight, cotangent, index, index, block_count, block_values[0, 0])


def solution(mesh):
    in_specs = (
        P(("col", "row"), None),
        P(),
        P(("row", "col"), None),
        P("row", "col", None),
        P("row", "col"),
        P("row", "col", None, None, None),
    )
    out_specs = (P(("row", "col"), None), P(("col", "row"), None), P())
    return jax.shard_map(body, mesh=mesh, in_specs=in_specs, out_specs=out_specs, check_vma=False)
```

```python
import functools
import math

import jax
import jax.numpy as jnp
from jax import lax
from jax.experimental import pallas as pl
from jax.experimental.pallas import tpu as pltpu
from jax.sharding import PartitionSpec as P

MESH = pl.DeviceIdType.MESH
BF = jnp.bfloat16
F32 = jnp.float32
RING = 4
ORDER = (2, 1, 3, 0)


def ids():
    table = {}

    def of(*key):
        return table.setdefault(key, len(table))

    return of


COPIES = 119


def kernel(
    feat_h, weight_h, cot_h, vals_h, idx_h, cnt,
    out_o, ig_o, wg_o,
    weight, vals, vals_t, fa, fa_t, ca, proj, run, pout, pback, tbl_v, tbl_s,
    rc, sy, own_y, ry, sz, rz, relay, rx, szl, rzl,
    wacc, wb, w1r, w3, w4, w5,
    idxs, ss, rs, ls, ins,
):
    of = ids()
    row = lax.axis_index("row")
    col = lax.axis_index("col")
    x, zl = row // 4, lax.rem(row, 4)
    y, zh, c = col // 8, lax.rem(col // 2, 4), lax.rem(col, 2)
    sib = 1 - c

    def r4(v):
        return lax.rem(v, 4)

    def dev(x_=x, zl_=zl, y_=y, zh_=zh, c_=c):
        return (x_ * 4 + zl_, y_ * 8 + zh_ * 2 + c_)

    def at(axis, k):
        here = {"x": x, "zl": zl, "y": y, "zh": zh}[axis]
        there = r4(here + k)
        return dev(**{axis + "_": there}), there

    sends = []
    def send(src, dst, key, device):
        n = of(*key)
        copy = pltpu.make_async_remote_copy(
            src_ref=src, dst_ref=dst, send_sem=ss.at[n], recv_sem=rs.at[n],
            device_id=device, device_id_type=MESH,
        )
        copy.start()
        sends.append(copy)

    def arrive(dst, key):
        n = of(*key)
        pltpu.make_async_remote_copy(
            src_ref=dst, dst_ref=dst, send_sem=ss.at[n], recv_sem=rs.at[n],
            device_id=dev(c_=sib), device_id_type=MESH,
        ).wait_recv()

    loads = [
        pltpu.make_async_copy(src, dst, ins.at[n])
        for n, (src, dst) in enumerate(
            [
                (feat_h, fa.at[row]), (cot_h, ca.at[col]), (weight_h, weight),
                (vals_h, vals), (idx_h, idxs),
            ]
        )
    ]
    for load in loads:
        load.start()

    barrier = pltpu.get_barrier_semaphore()
    partners = [at(a, k)[0] for a in ("x", "zl", "y", "zh") for k in (1, 2, 3)]
    partners.append(dev(c_=sib))
    shifts = [(kx, ky) for kx in (1, 3, 2, 0) for ky in (1, 3, 2, 0) if kx or ky]
    plane = {
        (kx, ky): dev(x_=r4(x + kx), y_=r4(y + ky)) for kx, ky in shifts
    }
    partners += [plane[kx, ky] for kx, ky in shifts if kx and ky]
    for p in partners:
        pl.semaphore_signal(barrier, inc=1, device_id=p, device_id_type=MESH)

    loads[0].wait()
    loads[1].wait()
    pl.semaphore_wait(barrier, len(partners))

    def features_on(block, tag):
        for k in (1, 2, 3):
            d, _ = at("x", k)
            send(fa.at[block], fa.at[block], ("fx", k, tag), d)

    def cotangents_on(block, tag):
        for k in (1, 2, 3):
            d, _ = at("y", k)
            send(ca.at[block], ca.at[block], ("cy", k, tag), d)
        send(ca.at[block], ca.at[block], ("cs", 0, tag), dev(c_=sib))

    for k in (1, 3):
        send(ca.at[col], ca.at[col], ("cz", k), at("zh", k)[0])
    for k in (1, 3, 2):
        send(fa.at[row], fa.at[row], ("fz", k), at("zl", k)[0])
    cotangents_on(col, 0)
    features_on(row, 0)

    for load in loads[2:]:
        load.wait()
    lane = lax.broadcasted_iota(jnp.int32, (1, 128), 1)
    count = cnt[0, 0]
    none = jnp.full((1, 128), 32, jnp.int32)
    zero = jnp.zeros((1, 128), jnp.int32)

    def place(t, carry):
        srow, scol = carry
        i = idxs[0, t]
        here = lane == t
        return jnp.where(here, i // 16, srow), jnp.where(here, lax.rem(i, 16), scol)

    srow, scol = lax.fori_loop(0, 32, place, (zero, zero))

    def link(t, carry):
        pf, lf, pb, lb = carry
        i = idxs[0, t]
        ti, tj = i // 16, lax.rem(i, 16)
        later = lane > t
        pf = jnp.where(later & (srow == ti), t, pf)
        pb = jnp.where(later & (scol == tj), t, pb)
        live = jnp.full((1, 128), t, jnp.int32) < count
        lf = jnp.where(live & (lane == ti), t, lf)
        lb = jnp.where(live & (lane == tj), t, lb)
        return pf, lf, pb, lb

    pf, lf, pb, lb = lax.fori_loop(0, 32, link, (none, none, none, none))
    for n, line in enumerate((scol, pf, lf, srow, pb, lb)):
        tbl_v[n : n + 1, :] = line
    table = pltpu.make_async_copy(tbl_v, tbl_s, ls)
    table.start()
    run[32] = jnp.zeros_like(run[32])

    def turn(s, carry):
        vals_t[s] = vals[s].T
        return carry

    def project(block):
        proj[block] = jnp.dot(fa[block], weight[...], preferred_element_type=F32).astype(BF)
        fa_t[block] = fa[block].T

    lax.fori_loop(0, 32, turn, 0, unroll=4)

    def features_in(k):
        block = x * 4 + r4(zl + 4 - k)
        arrive(fa.at[block], ("fz", k))
        features_on(block, k)

    far = y * 8 + r4(zh + 2) * 2 + c
    halves = (pl.ds(0, 64), pl.ds(64, 64))
    for n, k in enumerate((1, 3)):
        block = y * 8 + r4(zh + 4 - k) * 2 + c
        arrive(ca.at[block], ("cz", k))
        half = ca.at[block, halves[n]]
        send(half, half, ("ch", n), at("zh", k)[0])
        cotangents_on(block, k)

    def across(tag):
        for k in (1, 3, 2):
            block = r4(y + 4 - k) * 8 + r4(zh + 4 - tag) * 2 + c
            arrive(ca.at[block], ("cy", k, tag))
            send(ca.at[block], ca.at[block], ("cs", k, tag), dev(c_=sib))

    across(0)
    for k in (1, 3, 2):
        features_in(k)
    for k in (0, 1, 3, 2):
        project(x * 4 + r4(zl + 4 - k))
    for n in (0, 1):
        arrive(ca.at[far, halves[n]], ("ch", n))
    cotangents_on(far, 2)
    across(1)
    across(3)
    for tag in (0, 1, 3, 2):
        for k in (1, 3, 2):
            block = r4(x + 4 - k) * 4 + r4(zl + 4 - tag)
            arrive(fa.at[block], ("fx", k, tag))
            project(block)
    table.wait()

    def chain(left, right, at_line, previous_line):
        def some(q, carry):
            products = [
                jnp.dot(left[q * 8 + u], right[tbl_s[at_line, q * 8 + u]], preferred_element_type=F32)
                for u in range(8)
            ]
            for u in range(8):
                run[q * 8 + u] = products[u] + run[tbl_s[previous_line, q * 8 + u]]
            return carry

        lax.fori_loop(0, 4, some, 0)

    chain(vals, proj, 0, 1)

    def forward_out(o, carry):
        r = lax.rem(o, 4) * 8 + lax.rem(o // 4, 4) * 2 + o // 16
        pout[o] = run[tbl_s[2, r]].astype(BF)
        return carry

    lax.fori_loop(0, 32, forward_out, 0)

    def group(g):
        return r4(zh + ORDER[g])

    for g in range(4):
        part = pl.ds(sib * 16 + group(g) * 4, 4)
        send(pout.at[part], rc.at[pl.ds(g * 4, 4)], ("oc", g), dev(c_=sib))

    def out_y(g):
        arrive(rc.at[pl.ds(g * 4, 4)], ("oc", g))
        for k in (2, 1, 3):
            d, there = at("y", k)
            own = pout[c * 16 + group(g) * 4 + there].astype(F32)
            sy[g * 3 + k - 1] = (own + rc[g * 4 + there].astype(F32)).astype(BF)
            send(sy.at[g * 3 + k - 1], ry.at[g * 3 + k - 1], ("oy", g, k), d)
        own_y[g] = pout[c * 16 + group(g) * 4 + y].astype(F32) + rc[g * 4 + y].astype(F32)

    across(2)
    out_y(0)
    out_y(1)

    def total_y(g):
        total = own_y[g]
        for k in (1, 2, 3):
            arrive(ry.at[g * 3 + k - 1], ("oy", g, k))
            total = total + ry[g * 3 + k - 1].astype(F32)
        return total

    def out_z(g):
        sz[g] = total_y(g).astype(BF)
        if g == 0:
            for n, k in enumerate((1, 3)):
                send(sz.at[0, halves[n]], relay.at[n], ("or", n), at("zh", k)[0])
            return
        n = g - 1
        arrive(relay.at[n], ("or", n))
        sz[g, halves[n], :] = (sz[g, halves[n], :].astype(F32) + relay[n].astype(F32)).astype(BF)
        send(sz.at[g], rz.at[n], ("oz", n), at("zh", ORDER[g])[0])

    def out_end():
        total = total_y(3)
        for n in range(2):
            arrive(rz.at[n], ("oz", n))
            total = total + rz[n].astype(F32)
        out_o[...] = total.astype(BF)

    for tag in (0, 1, 3, 2):
        for k in (0, 1, 3, 2):
            block = r4(y + 4 - k) * 8 + r4(zh + 4 - tag) * 2 + sib
            arrive(ca.at[block], ("cs", k, tag))

    chain(vals_t, ca, 3, 4)

    def backward_out(j, carry):
        pback[j] = run[tbl_s[5, j]].astype(BF)
        return carry

    lax.fori_loop(0, 16, backward_out, 0)

    term = jnp.zeros((256, 256), F32)
    for j in range(16):
        term += jnp.dot(fa_t[j], pback[j], preferred_element_type=F32)
    wacc[...] = term
    wb[...] = term.astype(BF)

    def piece(x_, y_):
        return pl.ds(pl.multiple_of(x_ * 64 + y_ * 16, 16), 16)

    for kx, ky in shifts:
        part = wb.at[piece(r4(x + kx), r4(y + ky))]
        send(part, w1r.at[kx * 4 + ky], ("w1", kx, ky), plane[kx, ky])

    def term_zl():
        small = wacc[piece(x, y), :]
        for kx, ky in shifts:
            arrive(w1r.at[kx * 4 + ky], ("w1", kx, ky))
            small = small + w1r[kx * 4 + ky].astype(F32)
        w3[zl] = small.astype(BF)
        for k in (2, 1, 3):
            send(w3.at[zl], w3.at[zl], ("w3", k), at("zl", k)[0])

    def four(ref):
        low = ref[0].astype(F32) + ref[1].astype(F32)
        return low + ref[2].astype(F32) + ref[3].astype(F32)

    def term_zh():
        for k in (1, 2, 3):
            arrive(w3.at[r4(zl + 4 - k)], ("w3", k))
        w4[zh] = four(w3).astype(BF)
        for k in (2, 1, 3):
            send(w4.at[zh], w4.at[zh], ("w4", k), at("zh", k)[0])

    def term_core():
        for k in (1, 2, 3):
            arrive(w4.at[r4(zh + 4 - k)], ("w4", k))
        w5[0] = four(w4)
        send(w5.at[0], w5.at[1], ("w5",), dev(c_=sib))

    def back_xy():
        arrive(w5.at[1], ("w5",))
        mine = wg_o.at[piece(x, y)]
        mine[...] = (w5[0] + w5[1]) * (1.0 / math.sqrt(65536))
        for kx, ky in shifts:
            send(mine, mine, ("w6", kx, ky), plane[kx, ky])

    def back_end():
        for kx, ky in shifts:
            arrive(wg_o.at[piece(r4(x + 4 - kx), r4(y + 4 - ky))], ("w6", kx, ky))

    def grad_x(g):
        zt = r4(zl + ORDER[g])
        for k in (2, 1, 3):
            d, there = at("x", k)
            send(pback.at[there * 4 + zt], rx.at[g * 3 + k - 1], ("bx", g, k), d)

    def total_x(g):
        total = pback[x * 4 + r4(zl + ORDER[g])].astype(F32)
        for k in (1, 2, 3):
            arrive(rx.at[g * 3 + k - 1], ("bx", g, k))
            total = total + rx[g * 3 + k - 1].astype(F32)
        return total

    def grad_z(g):
        szl[g] = total_x(g).astype(BF)
        send(szl.at[g], rzl.at[g], ("bz", g), at("zl", ORDER[g])[0])

    def grad_end():
        grad = total_x(3)
        for g in range(3):
            arrive(rzl.at[g], ("bz", g))
            grad = grad + rzl[g].astype(F32)
        high = grad.astype(BF)
        low = (grad - high.astype(F32)).astype(BF)
        nt = (((1,), (1,)), ((), ()))
        ig_o[...] = (
            lax.dot_general(high, weight[...], nt, preferred_element_type=F32)
            + lax.dot_general(low, weight[...], nt, preferred_element_type=F32)
        ).astype(BF)

    out_y(2)
    out_y(3)
    for g in range(4):
        grad_x(g)
    out_z(0)
    term_zl()
    term_zh()
    out_z(1)
    out_z(2)
    grad_z(0)
    grad_z(1)
    grad_z(2)
    term_core()
    back_xy()
    out_end()
    grad_end()
    back_end()

    for copy in sends:
        copy.wait_send()


def body(features, weight, cotangent, block_index, block_count, block_values):
    hbm = pl.BlockSpec(memory_space=pltpu.HBM)
    index = block_index.reshape(1, 32)
    operands = [
        pltpu.with_memory_space_constraint(a, pltpu.HBM)
        for a in (features, weight, cotangent, block_values.reshape(32, 128, 128), index)
    ]
    blocks = functools.partial(lambda dtype, n: pltpu.VMEM((n, 128, 256), dtype))
    shapes = (
        jax.ShapeDtypeStruct((128, 256), BF),
        jax.ShapeDtypeStruct((128, 256), BF),
        jax.ShapeDtypeStruct((256, 256), F32),
    )
    vmem = pl.BlockSpec(memory_space=pltpu.VMEM)
    return pl.pallas_call(
        kernel,
        out_shape=shapes,
        in_specs=[hbm] * 5 + [pl.BlockSpec(memory_space=pltpu.SMEM)],
        out_specs=(vmem, vmem, vmem),
        scratch_shapes=[
            pltpu.VMEM((256, 256), BF), pltpu.VMEM((32, 128, 128), BF), pltpu.VMEM((32, 128, 128), BF),
            blocks(BF, 16), pltpu.VMEM((16, 256, 128), BF), blocks(BF, 32), blocks(BF, 16), blocks(F32, 33),
            blocks(BF, 32), blocks(BF, 16),
            pltpu.VMEM((8, 128), jnp.int32), pltpu.SMEM((8, 128), jnp.int32),
            blocks(BF, 16), blocks(BF, 12), blocks(F32, 4), blocks(BF, 12),
            blocks(BF, 3), blocks(BF, 2), pltpu.VMEM((2, 64, 256), BF), blocks(BF, 12), blocks(BF, 3), blocks(BF, 3),
            pltpu.VMEM((256, 256), F32), pltpu.VMEM((256, 256), BF), pltpu.VMEM((16, 16, 256), BF),
            pltpu.VMEM((4, 16, 256), BF), pltpu.VMEM((4, 16, 256), BF), pltpu.VMEM((2, 16, 256), F32),
            pltpu.SMEM((1, 32), jnp.int32),
            pltpu.SemaphoreType.DMA((COPIES,)), pltpu.SemaphoreType.DMA((COPIES,)),
            pltpu.SemaphoreType.DMA, pltpu.SemaphoreType.DMA((5,)),
        ],
        compiler_params=pltpu.CompilerParams(
            collective_id=0, has_side_effects=True, vmem_limit_bytes=48 << 20
        ),
        name="graph_step",
    )(*operands, block_count)


def solution(mesh):
    in_specs = (
        P(("col", "row"), None),
        P(),
        P(("row", "col"), None),
        P("row", "col", None),
        P("row", "col"),
        P("row", "col", None, None, None),
    )
    out_specs = (P(("row", "col"), None), P(("col", "row"), None), P())
    return jax.shard_map(body, mesh=mesh, in_specs=in_specs, out_specs=out_specs, check_vma=False)
```

```python
import functools
import math

import jax
import jax.numpy as jnp
from jax import lax
from jax.experimental import pallas as pl
from jax.experimental.pallas import tpu as pltpu
from jax.sharding import PartitionSpec as P

MESH = pl.DeviceIdType.MESH
BF = jnp.bfloat16
F32 = jnp.float32
RING = 4
ORDER = (2, 1, 3, 0)


def ids():
    table = {}

    def of(*key):
        n = table.setdefault(key, len(table))
        assert n < KEYS
        return n

    return of


KEYS = 37


def kernel(
    feat_h, weight_h, cot_h, vals_h, idx_h, cnt,
    out_o, ig_o, wg_o,
    weight, vals, vals_t, fa, fa_t, ca, proj, run, pout, pback, tbl_v, tbl_s,
    rc, sy, own_y, ry, sz, rz, relay, rx, szl, rzl,
    wacc, wb, w0r, wh, w1s, w1r, w3, w6, w8r,
    idxs, ss, rs, ls, ins, near,
):
    of = ids()
    row = lax.axis_index("row")
    col = lax.axis_index("col")
    x, zl = row // 4, lax.rem(row, 4)
    y, zh, c = col // 8, lax.rem(col // 2, 4), lax.rem(col, 2)
    sib = 1 - c

    def r4(v):
        return lax.rem(v, 4)

    def dev(x_=x, zl_=zl, y_=y, zh_=zh, c_=c):
        return (x_ * 4 + zl_, y_ * 8 + zh_ * 2 + c_)

    def at(axis, k):
        here = {"x": x, "zl": zl, "y": y, "zh": zh}[axis]
        there = r4(here + k)
        return dev(**{axis + "_": there}), there

    def send(src, dst, key, device, group=0):
        pltpu.make_async_remote_copy(
            src_ref=src, dst_ref=dst, send_sem=ss.at[group], recv_sem=rs.at[of(*key)],
            device_id=device, device_id_type=MESH,
        ).start()

    def arrive(ref, key):
        pltpu.make_async_remote_copy(
            src_ref=ref, dst_ref=ref, send_sem=ss.at[0], recv_sem=rs.at[of(*key)],
            device_id=dev(c_=sib), device_id_type=MESH,
        ).wait_recv()

    def sent(ref, group):
        pltpu.make_async_remote_copy(
            src_ref=ref, dst_ref=ref, send_sem=ss.at[group], recv_sem=rs.at[0],
            device_id=dev(c_=sib), device_id_type=MESH,
        ).wait_send()

    loads = [
        pltpu.make_async_copy(src, dst, ins.at[n])
        for n, (src, dst) in enumerate(
            [
                (feat_h, fa.at[row]), (cot_h, ca.at[col]), (weight_h, weight),
                (vals_h, vals), (idx_h, idxs),
            ]
        )
    ]
    for load in loads:
        load.start()

    barrier = pltpu.get_barrier_semaphore()
    x_peers, zl_peers, y_peers = ([at(a, k)[0] for k in (1, 2, 3)] for a in ("x", "zl", "y"))
    zh_peers = [at("zh", k)[0] for k in (1, 3)]
    partners = [*x_peers, *zl_peers, *y_peers, *zh_peers, dev(c_=sib)]
    for p in partners:
        pl.semaphore_signal(barrier, inc=1, device_id=p, device_id_type=MESH)

    loads[0].wait()
    loads[1].wait()
    pl.semaphore_wait(barrier, len(partners))

    def tell(n, devices):
        for p in devices:
            pl.semaphore_signal(near.at[n], inc=1, device_id=p, device_id_type=MESH)

    tell(0, zh_peers)
    tell(2, x_peers)
    shifts = [(a, b) for a in (1, 3, 2, 0) for b in (1, 3, 2, 0) if a or b]

    def features_on(block, tag):
        for k in (1, 2, 3):
            d, _ = at("x", k)
            send(fa.at[block], fa.at[block], ("fx", tag), d)

    def cotangents_on(block, tag):
        for k in (1, 2, 3):
            d, _ = at("y", k)
            send(ca.at[block], ca.at[block], ("cy", tag), d)
        send(ca.at[block], ca.at[block], ("cs",), dev(c_=sib))

    for k in (1, 3):
        send(ca.at[col], ca.at[col], ("cz", k), at("zh", k)[0])
    for k in (1, 3, 2):
        send(fa.at[row], fa.at[row], ("fz", k), at("zl", k)[0])
    cotangents_on(col, 0)
    features_on(row, 0)

    for load in loads[2:]:
        load.wait()
    lane = lax.broadcasted_iota(jnp.int32, (1, 128), 1)
    count = cnt[0, 0]
    none = jnp.full((1, 128), 32, jnp.int32)
    zero = jnp.zeros((1, 128), jnp.int32)

    def place(t, carry):
        srow, scol = carry
        i = idxs[0, t]
        here = lane == t
        return jnp.where(here, i // 16, srow), jnp.where(here, lax.rem(i, 16), scol)

    srow, scol = lax.fori_loop(0, 32, place, (zero, zero))

    def link(t, carry):
        pf, lf, pb, lb = carry
        i = idxs[0, t]
        ti, tj = i // 16, lax.rem(i, 16)
        later = lane > t
        pf = jnp.where(later & (srow == ti), t, pf)
        pb = jnp.where(later & (scol == tj), t, pb)
        live = jnp.full((1, 128), t, jnp.int32) < count
        lf = jnp.where(live & (lane == ti), t, lf)
        lb = jnp.where(live & (lane == tj), t, lb)
        return pf, lf, pb, lb

    pf, lf, pb, lb = lax.fori_loop(0, 32, link, (none, none, none, none))
    for n, line in enumerate((scol, pf, lf, srow, pb, lb)):
        tbl_v[n : n + 1, :] = line
    table = pltpu.make_async_copy(tbl_v, tbl_s, ls)
    table.start()
    run[32] = jnp.zeros_like(run[32])

    def turn(s, carry):
        vals_t[s] = vals[s].T
        return carry

    def project(block):
        proj[block] = jnp.dot(fa[block], weight[...], preferred_element_type=F32).astype(BF)
        fa_t[block] = fa[block].T

    lax.fori_loop(0, 32, turn, 0, unroll=4)

    def features_in(k):
        block = x * 4 + r4(zl + 4 - k)
        arrive(fa.at[block], ("fz", k))
        features_on(block, k)

    far = y * 8 + r4(zh + 2) * 2 + c
    halves = (pl.ds(0, 64), pl.ds(64, 64))
    for n, k in enumerate((1, 3)):
        block = y * 8 + r4(zh + 4 - k) * 2 + c
        arrive(ca.at[block], ("cz", k))
        half = ca.at[block, halves[n]]
        send(half, half, ("ch",), at("zh", k)[0])
        cotangents_on(block, k)

    def across(tag):
        arrive(ca.at[pl.ds(0, 3)], ("cy", tag))
        for k in (1, 3, 2):
            block = r4(y + 4 - k) * 8 + r4(zh + 4 - tag) * 2 + c
            send(ca.at[block], ca.at[block], ("cs",), dev(c_=sib))

    pl.semaphore_wait(near.at[0], 2)
    tell(1, zl_peers)
    across(0)
    for k in (1, 3, 2):
        features_in(k)
    for k in (0, 1, 3, 2):
        project(x * 4 + r4(zl + 4 - k))
    arrive(ca.at[far], ("ch",))
    cotangents_on(far, 2)
    across(1)
    across(3)
    for tag in (0, 1, 3, 2):
        arrive(fa.at[pl.ds(0, 3)], ("fx", tag))
        for k in (1, 3, 2):
            project(r4(x + 4 - k) * 4 + r4(zl + 4 - tag))
    table.wait()

    def chain(left, right, at_line, previous_line):
        def some(q, carry):
            products = [
                jnp.dot(left[q * 8 + u], right[tbl_s[at_line, q * 8 + u]], preferred_element_type=F32)
                for u in range(8)
            ]
            for u in range(8):
                run[q * 8 + u] = products[u] + run[tbl_s[previous_line, q * 8 + u]]
            return carry

        lax.fori_loop(0, 4, some, 0)

    chain(vals, proj, 0, 1)

    def forward_out(o, carry):
        r = lax.rem(o, 4) * 8 + lax.rem(o // 4, 4) * 2 + o // 16
        pout[o] = run[tbl_s[2, r]].astype(BF)
        return carry

    lax.fori_loop(0, 32, forward_out, 0)

    def group(g):
        return r4(zh + ORDER[g])

    for g in range(4):
        part = pl.ds(sib * 16 + group(g) * 4, 4)
        send(pout.at[part], rc.at[pl.ds(g * 4, 4)], ("oc", g), dev(c_=sib), 1)

    def out_y(g):
        arrive(rc.at[pl.ds(g * 4, 4)], ("oc", g))
        for k in (2, 1, 3):
            d, there = at("y", k)
            own = pout[c * 16 + group(g) * 4 + there].astype(F32)
            sy[g * 3 + k - 1] = (own + rc[g * 4 + there].astype(F32)).astype(BF)
            send(sy.at[g * 3 + k - 1], ry.at[g * 3 + k - 1], ("oy", g), d, 1)
        own_y[g] = pout[c * 16 + group(g) * 4 + y].astype(F32) + rc[g * 4 + y].astype(F32)

    across(2)
    out_y(0)
    out_y(1)

    def total_y(g):
        total = own_y[g]
        arrive(ry.at[pl.ds(g * 3, 3)], ("oy", g))
        for k in (1, 2, 3):
            total = total + ry[g * 3 + k - 1].astype(F32)
        return total

    def out_z(g):
        sz[g] = total_y(g).astype(BF)
        if g == 0:
            for n, k in enumerate((1, 3)):
                send(sz.at[0, halves[n]], relay.at[n], ("or", n), at("zh", k)[0], 1)
            return
        n = g - 1
        arrive(relay.at[n], ("or", n))
        sz[g, halves[n], :] = (sz[g, halves[n], :].astype(F32) + relay[n].astype(F32)).astype(BF)
        send(sz.at[g], rz.at[n], ("oz",), at("zh", ORDER[g])[0], 1)

    def out_end():
        total = total_y(3)
        arrive(rz, ("oz",))
        for n in range(2):
            total = total + rz[n].astype(F32)
        out_o[...] = total.astype(BF)

    arrive(ca.at[pl.ds(0, 16)], ("cs",))

    chain(vals_t, ca, 3, 4)

    def backward_out(j, carry):
        pback[j] = run[tbl_s[5, j]].astype(BF)
        return carry

    lax.fori_loop(0, 16, backward_out, 0)

    term = jnp.zeros((256, 256), F32)
    for j in range(16):
        term += jnp.dot(fa_t[j], pback[j], preferred_element_type=F32)
    wacc[...] = term
    wb[...] = term.astype(BF)
    send(wb.at[pl.ds(pl.multiple_of(sib * 128, 128), 128)], w0r, ("w0",), dev(c_=sib), 2)

    def term_xy():
        arrive(w0r, ("w0",))
        half = wacc[pl.ds(pl.multiple_of(c * 128, 128), 128), :] + w0r[...].astype(F32)
        for p in range(16):
            piece = half[p // 2 * 16 : p // 2 * 16 + 16, p % 2 * 128 : p % 2 * 128 + 128]
            wh[p] = piece
            w1s[p] = piece.astype(BF)
        pl.semaphore_wait(near.at[2], 3)
        for kx, ky in shifts:
            there_x, there_y = r4(x + kx), r4(y + ky)
            send(
                w1s.at[there_x * 4 + there_y], w1r.at[kx * 4 + ky - 1], ("w1",),
                dev(x_=there_x, y_=there_y), 3,
            )

    def term_z():
        arrive(w1r, ("w1",))
        small = wh[x * 4 + y]
        for n in range(15):
            small = small + w1r[n].astype(F32)
        mine = w3.at[zl * 4 + zh]
        mine[...] = small.astype(BF)
        pl.semaphore_wait(near.at[1], 3)
        for kl, kh in shifts:
            send(mine, mine, ("w3",), dev(zl_=r4(zl + kl), zh_=r4(zh + kh)), 4)

    def back_xy():
        arrive(w3.at[pl.ds(0, 15)], ("w3",))
        total = w3[0].astype(F32)
        for n in range(1, 16):
            total = total + w3[n].astype(F32)
        mine = w6.at[x * 4 + y]
        mine[...] = (total * (1.0 / math.sqrt(65536))).astype(BF)
        for kx, ky in shifts:
            send(mine, mine, ("w6",), dev(x_=r4(x + kx), y_=r4(y + ky)), 5)

    def back_core():
        arrive(w6.at[pl.ds(0, 15)], ("w6",))
        send(w6, w8r, ("w8",), dev(c_=sib), 2)

    def back_end():
        for here, ref in ((c, w6), (sib, w8r)):
            if ref is w8r:
                arrive(w8r, ("w8",))
            for p in range(16):
                at_row = pl.multiple_of(here * 128 + p // 2 * 16, 16)
                wg_o[pl.ds(at_row, 16), p % 2 * 128 : p % 2 * 128 + 128] = ref[p].astype(F32)

    def grad_x(g):
        zt = r4(zl + ORDER[g])
        for k in (2, 1, 3):
            d, there = at("x", k)
            send(pback.at[there * 4 + zt], rx.at[g * 3 + k - 1], ("bx", g), d, 1)

    def total_x(g):
        total = pback[x * 4 + r4(zl + ORDER[g])].astype(F32)
        arrive(rx.at[pl.ds(g * 3, 3)], ("bx", g))
        for k in (1, 2, 3):
            total = total + rx[g * 3 + k - 1].astype(F32)
        return total

    def grad_z(g):
        szl[g] = total_x(g).astype(BF)
        send(szl.at[g], rzl.at[g], ("bz",), at("zl", ORDER[g])[0], 1)

    def grad_end():
        grad = total_x(3)
        arrive(rzl, ("bz",))
        for g in range(3):
            grad = grad + rzl[g].astype(F32)
        high = grad.astype(BF)
        low = (grad - high.astype(F32)).astype(BF)
        nt = (((1,), (1,)), ((), ()))
        ig_o[...] = (
            lax.dot_general(high, weight[...], nt, preferred_element_type=F32)
            + lax.dot_general(low, weight[...], nt, preferred_element_type=F32)
        ).astype(BF)

    term_xy()
    out_y(2)
    out_y(3)
    for g in range(4):
        grad_x(g)
    out_z(0)
    term_z()
    out_z(1)
    out_z(2)
    grad_z(0)
    grad_z(1)
    grad_z(2)
    back_xy()
    out_end()
    back_core()
    grad_end()
    back_end()

    for group, ref in enumerate((run.at[pl.ds(0, 23)], run.at[pl.ds(0, 23)], fa.at[pl.ds(0, 2)], w1r, w1r, w1r)):
        sent(ref, group)


def body(features, weight, cotangent, block_index, block_count, block_values):
    hbm = pl.BlockSpec(memory_space=pltpu.HBM)
    index = block_index.reshape(1, 32)
    operands = [
        pltpu.with_memory_space_constraint(a, pltpu.HBM)
        for a in (features, weight, cotangent, block_values.reshape(32, 128, 128), index)
    ]
    blocks = functools.partial(lambda dtype, n: pltpu.VMEM((n, 128, 256), dtype))
    shapes = (
        jax.ShapeDtypeStruct((128, 256), BF),
        jax.ShapeDtypeStruct((128, 256), BF),
        jax.ShapeDtypeStruct((256, 256), F32),
    )
    vmem = pl.BlockSpec(memory_space=pltpu.VMEM)
    return pl.pallas_call(
        kernel,
        out_shape=shapes,
        in_specs=[hbm] * 5 + [pl.BlockSpec(memory_space=pltpu.SMEM)],
        out_specs=(vmem, vmem, vmem),
        scratch_shapes=[
            pltpu.VMEM((256, 256), BF), pltpu.VMEM((32, 128, 128), BF), pltpu.VMEM((32, 128, 128), BF),
            blocks(BF, 16), pltpu.VMEM((16, 256, 128), BF), blocks(BF, 32), blocks(BF, 16), blocks(F32, 33),
            blocks(BF, 32), blocks(BF, 16),
            pltpu.VMEM((8, 128), jnp.int32), pltpu.SMEM((8, 128), jnp.int32),
            blocks(BF, 16), blocks(BF, 12), blocks(F32, 4), blocks(BF, 12),
            blocks(BF, 3), blocks(BF, 2), pltpu.VMEM((2, 64, 256), BF), blocks(BF, 12), blocks(BF, 3), blocks(BF, 3),
            pltpu.VMEM((256, 256), F32), pltpu.VMEM((256, 256), BF), pltpu.VMEM((128, 256), BF),
            pltpu.VMEM((16, 16, 128), F32), *(pltpu.VMEM((n, 16, 128), BF) for n in (16, 15, 16, 16, 16)),
            pltpu.SMEM((1, 32), jnp.int32),
            pltpu.SemaphoreType.DMA((6,)), pltpu.SemaphoreType.DMA((KEYS,)),
            pltpu.SemaphoreType.DMA, pltpu.SemaphoreType.DMA((5,)), pltpu.SemaphoreType.REGULAR((3,)),
        ],
        compiler_params=pltpu.CompilerParams(
            collective_id=0, has_side_effects=True, vmem_limit_bytes=48 << 20
        ),
        name="graph_step",
    )(*operands, block_count)


def solution(mesh):
    in_specs = (
        P(("col", "row"), None),
        P(),
        P(("row", "col"), None),
        P("row", "col", None),
        P("row", "col"),
        P("row", "col", None, None, None),
    )
    out_specs = (P(("row", "col"), None), P(("col", "row"), None), P())
    return jax.shard_map(body, mesh=mesh, in_specs=in_specs, out_specs=out_specs, check_vma=False)
```

```python
import functools
import math

import jax
import jax.numpy as jnp
from jax import lax
from jax.experimental import pallas as pl
from jax.experimental.pallas import tpu as pltpu
from jax.sharding import PartitionSpec as P

MESH = pl.DeviceIdType.MESH
BF = jnp.bfloat16
F32 = jnp.float32
RING = 4
ORDER = (2, 1, 3, 0)


def ids():
    table = {}

    def of(*key):
        n = table.setdefault(key, len(table))
        assert n < KEYS
        return n

    return of


KEYS = 37


def kernel(
    feat_h, weight_h, cot_h, vals_h, idx_h, cnt,
    out_o, ig_o, wg_o,
    weight, vals, vals_t, fa, fa_t, ca, proj, run, pout, pback, tbl_v, tbl_s,
    rc, sy, own_y, ry, sz, rz, relay, rx, szl, rzl,
    wacc, wb, w0r, wh, w1s, w1r, w3, w6, w8r,
    idxs, ss, rs, ls, ins, near,
):
    of = ids()
    row = lax.axis_index("row")
    col = lax.axis_index("col")
    x, zl = row // 4, lax.rem(row, 4)
    y, zh, c = col // 8, lax.rem(col // 2, 4), lax.rem(col, 2)
    sib = 1 - c

    def r4(v):
        return lax.rem(v, 4)

    def dev(x_=x, zl_=zl, y_=y, zh_=zh, c_=c):
        return (x_ * 4 + zl_, y_ * 8 + zh_ * 2 + c_)

    def at(axis, k):
        here = {"x": x, "zl": zl, "y": y, "zh": zh}[axis]
        there = r4(here + k)
        return dev(**{axis + "_": there}), there

    def send(src, dst, key, device, group=0):
        pltpu.make_async_remote_copy(
            src_ref=src, dst_ref=dst, send_sem=ss.at[group], recv_sem=rs.at[of(*key)],
            device_id=device, device_id_type=MESH,
        ).start()

    def arrive(ref, key):
        pltpu.make_async_remote_copy(
            src_ref=ref, dst_ref=ref, send_sem=ss.at[0], recv_sem=rs.at[of(*key)],
            device_id=dev(c_=sib), device_id_type=MESH,
        ).wait_recv()

    def sent(ref, group):
        pltpu.make_async_remote_copy(
            src_ref=ref, dst_ref=ref, send_sem=ss.at[group], recv_sem=rs.at[0],
            device_id=dev(c_=sib), device_id_type=MESH,
        ).wait_send()

    loads = [
        pltpu.make_async_copy(src, dst, ins.at[n])
        for n, (src, dst) in enumerate(
            [
                (feat_h, fa.at[row]), (cot_h, ca.at[col]), (weight_h, weight),
                (vals_h, vals), (idx_h, idxs),
            ]
        )
    ]
    for load in loads:
        load.start()

    barrier = pltpu.get_barrier_semaphore()
    x_peers, zl_peers, y_peers = ([at(a, k)[0] for k in (1, 2, 3)] for a in ("x", "zl", "y"))
    zh_peers = [at("zh", k)[0] for k in (1, 3)]
    partners = [*x_peers, *zl_peers, *y_peers, *zh_peers, dev(c_=sib)]
    for p in partners:
        pl.semaphore_signal(barrier, inc=1, device_id=p, device_id_type=MESH)

    loads[0].wait()
    loads[1].wait()
    pl.semaphore_wait(barrier, len(partners))

    def tell(n, devices):
        for p in devices:
            pl.semaphore_signal(near.at[n], inc=1, device_id=p, device_id_type=MESH)

    tell(0, zh_peers)
    tell(2, x_peers)
    shifts = [(a, b) for a in (1, 3, 2, 0) for b in (1, 3, 2, 0) if a or b]

    def features_on(block, tag):
        for k in (1, 2, 3):
            d, _ = at("x", k)
            send(fa.at[block], fa.at[block], ("fx", tag), d)

    def cotangents_on(block, tag):
        for k in (1, 2, 3):
            d, _ = at("y", k)
            send(ca.at[block], ca.at[block], ("cy", tag), d)
        send(ca.at[block], ca.at[block], ("cs",), dev(c_=sib))

    for k in (1, 3):
        send(ca.at[col], ca.at[col], ("cz", k), at("zh", k)[0])
    for k in (1, 3):
        send(fa.at[row], fa.at[row], ("fz", k), at("zl", k)[0])
    cotangents_on(col, 0)
    features_on(row, 0)

    for load in loads[2:]:
        load.wait()
    lane = lax.broadcasted_iota(jnp.int32, (1, 128), 1)
    count = cnt[0, 0]
    none = jnp.full((1, 128), 32, jnp.int32)
    zero = jnp.zeros((1, 128), jnp.int32)

    def place(t, carry):
        srow, scol = carry
        i = idxs[0, t]
        here = lane == t
        return jnp.where(here, i // 16, srow), jnp.where(here, lax.rem(i, 16), scol)

    srow, scol = lax.fori_loop(0, 32, place, (zero, zero))

    def link(t, carry):
        pf, lf, pb, lb = carry
        i = idxs[0, t]
        ti, tj = i // 16, lax.rem(i, 16)
        later = lane > t
        pf = jnp.where(later & (srow == ti), t, pf)
        pb = jnp.where(later & (scol == tj), t, pb)
        live = jnp.full((1, 128), t, jnp.int32) < count
        lf = jnp.where(live & (lane == ti), t, lf)
        lb = jnp.where(live & (lane == tj), t, lb)
        return pf, lf, pb, lb

    pf, lf, pb, lb = lax.fori_loop(0, 32, link, (none, none, none, none))
    for n, line in enumerate((scol, pf, lf, srow, pb, lb)):
        tbl_v[n : n + 1, :] = line
    table = pltpu.make_async_copy(tbl_v, tbl_s, ls)
    table.start()
    run[32] = jnp.zeros_like(run[32])

    def turn(s, carry):
        vals_t[s] = vals[s].T
        return carry

    def project(block):
        proj[block] = jnp.dot(fa[block], weight[...], preferred_element_type=F32).astype(BF)
        fa_t[block] = fa[block].T

    lax.fori_loop(0, 32, turn, 0, unroll=4)

    def features_in(k):
        block = x * 4 + r4(zl + 4 - k)
        arrive(fa.at[block], ("fz", k))
        features_on(block, k)

    far = y * 8 + r4(zh + 2) * 2 + c
    halves = (pl.ds(0, 64), pl.ds(64, 64))
    for n, k in enumerate((1, 3)):
        block = y * 8 + r4(zh + 4 - k) * 2 + c
        arrive(ca.at[block], ("cz", k))
        half = ca.at[block, halves[n]]
        send(half, half, ("ch",), at("zh", k)[0])
        cotangents_on(block, k)

    def across(tag):
        arrive(ca.at[pl.ds(0, 3)], ("cy", tag))
        for k in (1, 3, 2):
            block = r4(y + 4 - k) * 8 + r4(zh + 4 - tag) * 2 + c
            send(ca.at[block], ca.at[block], ("cs",), dev(c_=sib))

    send(fa.at[row], fa.at[row], ("fz", 2), at("zl", 2)[0])
    pl.semaphore_wait(near.at[0], 2)
    tell(1, zl_peers)
    across(0)
    for k in (1, 3, 2):
        features_in(k)
    for k in (0, 1, 3, 2):
        project(x * 4 + r4(zl + 4 - k))
    arrive(ca.at[far], ("ch",))
    cotangents_on(far, 2)
    across(1)
    across(3)
    for tag in (0, 1, 3, 2):
        arrive(fa.at[pl.ds(0, 3)], ("fx", tag))
        for k in (1, 3, 2):
            project(r4(x + 4 - k) * 4 + r4(zl + 4 - tag))
    table.wait()

    def chain(left, right, at_line, previous_line):
        def some(q, carry):
            products = [
                jnp.dot(left[q * 8 + u], right[tbl_s[at_line, q * 8 + u]], preferred_element_type=F32)
                for u in range(8)
            ]
            for u in range(8):
                run[q * 8 + u] = products[u] + run[tbl_s[previous_line, q * 8 + u]]
            return carry

        lax.fori_loop(0, 4, some, 0)

    chain(vals, proj, 0, 1)

    def forward_out(o, carry):
        r = lax.rem(o, 4) * 8 + lax.rem(o // 4, 4) * 2 + o // 16
        pout[o] = run[tbl_s[2, r]].astype(BF)
        return carry

    lax.fori_loop(0, 32, forward_out, 0)

    def group(g):
        return r4(zh + ORDER[g])

    for g in range(4):
        part = pl.ds(sib * 16 + group(g) * 4, 4)
        send(pout.at[part], rc.at[pl.ds(g * 4, 4)], ("oc", g), dev(c_=sib), 1)

    def out_y(g):
        arrive(rc.at[pl.ds(g * 4, 4)], ("oc", g))
        for k in (2, 1, 3):
            d, there = at("y", k)
            own = pout[c * 16 + group(g) * 4 + there].astype(F32)
            sy[g * 3 + k - 1] = (own + rc[g * 4 + there].astype(F32)).astype(BF)
            send(sy.at[g * 3 + k - 1], ry.at[g * 3 + k - 1], ("oy", g), d, 1)
        own_y[g] = pout[c * 16 + group(g) * 4 + y].astype(F32) + rc[g * 4 + y].astype(F32)

    across(2)
    out_y(0)
    out_y(1)

    def total_y(g):
        total = own_y[g]
        arrive(ry.at[pl.ds(g * 3, 3)], ("oy", g))
        for k in (1, 2, 3):
            total = total + ry[g * 3 + k - 1].astype(F32)
        return total

    def out_z(g):
        sz[g] = total_y(g).astype(BF)
        if g == 0:
            for n, k in enumerate((1, 3)):
                send(sz.at[0, halves[n]], relay.at[n], ("or", n), at("zh", k)[0], 1)
            return
        n = g - 1
        arrive(relay.at[n], ("or", n))
        sz[g, halves[n], :] = (sz[g, halves[n], :].astype(F32) + relay[n].astype(F32)).astype(BF)
        send(sz.at[g], rz.at[n], ("oz",), at("zh", ORDER[g])[0], 1)

    def out_end():
        total = total_y(3)
        arrive(rz, ("oz",))
        for n in range(2):
            total = total + rz[n].astype(F32)
        out_o[...] = total.astype(BF)

    arrive(ca.at[pl.ds(0, 16)], ("cs",))

    chain(vals_t, ca, 3, 4)

    def backward_out(j, carry):
        pback[j] = run[tbl_s[5, j]].astype(BF)
        return carry

    lax.fori_loop(0, 16, backward_out, 0)

    term = jnp.zeros((256, 256), F32)
    for j in range(16):
        term += jnp.dot(fa_t[j], pback[j], preferred_element_type=F32)
    wacc[...] = term
    wb[...] = term.astype(BF)
    send(wb.at[pl.ds(pl.multiple_of(sib * 128, 128), 128)], w0r, ("w0",), dev(c_=sib), 2)

    def term_xy():
        arrive(w0r, ("w0",))
        half = wacc[pl.ds(pl.multiple_of(c * 128, 128), 128), :] + w0r[...].astype(F32)
        for p in range(16):
            piece = half[p // 2 * 16 : p // 2 * 16 + 16, p % 2 * 128 : p % 2 * 128 + 128]
            wh[p] = piece
            w1s[p] = piece.astype(BF)
        pl.semaphore_wait(near.at[2], 3)
        for kx, ky in shifts:
            there_x, there_y = r4(x + kx), r4(y + ky)
            send(
                w1s.at[there_x * 4 + there_y], w1r.at[kx * 4 + ky - 1], ("w1",),
                dev(x_=there_x, y_=there_y), 3,
            )

    def term_z():
        arrive(w1r, ("w1",))
        small = wh[x * 4 + y]
        for n in range(15):
            small = small + w1r[n].astype(F32)
        mine = w3.at[zl * 4 + zh]
        mine[...] = small.astype(BF)
        pl.semaphore_wait(near.at[1], 3)
        for kl, kh in shifts:
            send(mine, mine, ("w3",), dev(zl_=r4(zl + kl), zh_=r4(zh + kh)), 4)

    def back_xy():
        arrive(w3.at[pl.ds(0, 15)], ("w3",))
        total = w3[0].astype(F32)
        for n in range(1, 16):
            total = total + w3[n].astype(F32)
        mine = w6.at[x * 4 + y]
        mine[...] = (total * (1.0 / math.sqrt(65536))).astype(BF)
        for kx, ky in shifts:
            send(mine, mine, ("w6",), dev(x_=r4(x + kx), y_=r4(y + ky)), 5)

    def back_core():
        arrive(w6.at[pl.ds(0, 15)], ("w6",))
        send(w6, w8r, ("w8",), dev(c_=sib), 2)

    def back_end():
        for here, ref in ((c, w6), (sib, w8r)):
            if ref is w8r:
                arrive(w8r, ("w8",))
            for p in range(16):
                at_row = pl.multiple_of(here * 128 + p // 2 * 16, 16)
                wg_o[pl.ds(at_row, 16), p % 2 * 128 : p % 2 * 128 + 128] = ref[p].astype(F32)

    def grad_x(g):
        zt = r4(zl + ORDER[g])
        for k in (2, 1, 3):
            d, there = at("x", k)
            send(pback.at[there * 4 + zt], rx.at[g * 3 + k - 1], ("bx", g), d, 1)

    def total_x(g):
        total = pback[x * 4 + r4(zl + ORDER[g])].astype(F32)
        arrive(rx.at[pl.ds(g * 3, 3)], ("bx", g))
        for k in (1, 2, 3):
            total = total + rx[g * 3 + k - 1].astype(F32)
        return total

    def grad_z(g):
        szl[g] = total_x(g).astype(BF)
        send(szl.at[g], rzl.at[g], ("bz",), at("zl", ORDER[g])[0], 1)

    def grad_end():
        grad = total_x(3)
        arrive(rzl, ("bz",))
        for g in range(3):
            grad = grad + rzl[g].astype(F32)
        high = grad.astype(BF)
        low = (grad - high.astype(F32)).astype(BF)
        nt = (((1,), (1,)), ((), ()))
        ig_o[...] = (
            lax.dot_general(high, weight[...], nt, preferred_element_type=F32)
            + lax.dot_general(low, weight[...], nt, preferred_element_type=F32)
        ).astype(BF)

    term_xy()
    tell(4, [dev(c_=sib)])
    pl.semaphore_wait(near.at[4], 1)
    out_y(2)
    grad_x(0)
    out_z(0)
    term_z()
    tell(3, [dev(c_=sib)])
    pl.semaphore_wait(near.at[3], 1)
    out_z(1)
    out_y(3)
    grad_x(1)
    grad_x(2)
    grad_x(3)
    out_z(2)
    back_xy()
    grad_z(0)
    grad_z(1)
    grad_z(2)
    out_end()
    back_core()
    grad_end()
    back_end()

    for group, ref in enumerate((run.at[pl.ds(0, 23)], run.at[pl.ds(0, 23)], fa.at[pl.ds(0, 2)], w1r, w1r, w1r)):
        sent(ref, group)


def hand_over(*refs):
    copies = [pltpu.make_async_copy(refs[n], refs[n + 3], refs[6].at[n]) for n in range(3)]
    for copy in copies:
        copy.start()
    for copy in copies:
        copy.wait()


def body(features, weight, cotangent, block_index, block_count, block_values):
    hbm = pl.BlockSpec(memory_space=pltpu.HBM)
    index = block_index.reshape(1, 32)
    operands = [
        pltpu.with_memory_space_constraint(a, pltpu.HBM)
        for a in (features, weight, cotangent, block_values.reshape(32, 128, 128), index)
    ]
    blocks = functools.partial(lambda dtype, n: pltpu.VMEM((n, 128, 256), dtype))
    shapes = (
        jax.ShapeDtypeStruct((128, 256), BF),
        jax.ShapeDtypeStruct((128, 256), BF),
        jax.ShapeDtypeStruct((256, 256), F32),
    )
    vmem = pl.BlockSpec(memory_space=pltpu.VMEM)
    results = pl.pallas_call(
        kernel,
        out_shape=shapes,
        in_specs=[hbm] * 5 + [pl.BlockSpec(memory_space=pltpu.SMEM)],
        out_specs=(vmem, vmem, vmem),
        scratch_shapes=[
            pltpu.VMEM((256, 256), BF), pltpu.VMEM((32, 128, 128), BF), pltpu.VMEM((32, 128, 128), BF),
            blocks(BF, 16), pltpu.VMEM((16, 256, 128), BF), blocks(BF, 32), blocks(BF, 16), blocks(F32, 33),
            blocks(BF, 32), blocks(BF, 16),
            pltpu.VMEM((8, 128), jnp.int32), pltpu.SMEM((8, 128), jnp.int32),
            blocks(BF, 16), blocks(BF, 12), blocks(F32, 4), blocks(BF, 12),
            blocks(BF, 3), blocks(BF, 2), pltpu.VMEM((2, 64, 256), BF), blocks(BF, 12), blocks(BF, 3), blocks(BF, 3),
            pltpu.VMEM((256, 256), F32), pltpu.VMEM((256, 256), BF), pltpu.VMEM((128, 256), BF),
            pltpu.VMEM((16, 16, 128), F32), *(pltpu.VMEM((n, 16, 128), BF) for n in (16, 15, 16, 16, 16)),
            pltpu.SMEM((1, 32), jnp.int32),
            pltpu.SemaphoreType.DMA((6,)), pltpu.SemaphoreType.DMA((KEYS,)),
            pltpu.SemaphoreType.DMA, pltpu.SemaphoreType.DMA((5,)), pltpu.SemaphoreType.REGULAR((5,)),
        ],
        compiler_params=pltpu.CompilerParams(
            collective_id=0, has_side_effects=True, vmem_limit_bytes=48 << 20
        ),
        name="graph_step",
    )(*operands, block_count)
    return pl.pallas_call(
        hand_over,
        out_shape=shapes,
        in_specs=[vmem] * 3,
        out_specs=(hbm, hbm, hbm),
        scratch_shapes=[pltpu.SemaphoreType.DMA((3,))],
        name="hand_over",
    )(*(pltpu.with_memory_space_constraint(r, pltpu.VMEM) for r in results))


def solution(mesh):
    in_specs = (
        P(("col", "row"), None),
        P(),
        P(("row", "col"), None),
        P("row", "col", None),
        P("row", "col"),
        P("row", "col", None, None, None),
    )
    out_specs = (P(("row", "col"), None), P(("col", "row"), None), P())
    return jax.shard_map(body, mesh=mesh, in_specs=in_specs, out_specs=out_specs, check_vma=False)
```

```python
import functools
import math

import jax
import jax.numpy as jnp
from jax import lax
from jax.experimental import pallas as pl
from jax.experimental.pallas import tpu as pltpu
from jax.sharding import PartitionSpec as P

MESH = pl.DeviceIdType.MESH
BF = jnp.bfloat16
F32 = jnp.float32
RING = 4
ORDER = (2, 1, 3, 0)


def ids():
    table = {}

    def of(*key):
        n = table.setdefault(key, len(table))
        assert n < KEYS
        return n

    return of


KEYS = 37


def kernel(
    feat_h, weight_h, cot_h, vals_h, idx_h, cnt,
    out_o, ig_o, wg_o,
    weight, vals, vals_t, fa, fa_t, ca, proj, run, pout, pback, tbl_v, tbl_s,
    rc, sy, own_y, ry, sz, rz, relay, rx, szl, rzl,
    wacc, wb, w0r, wh, w1s, w1r, w3, w6, w8r,
    idxs, ss, rs, ls, ins, near,
):
    of = ids()
    row = lax.axis_index("row")
    col = lax.axis_index("col")
    x, zl = row // 4, lax.rem(row, 4)
    y, zh, c = col // 8, lax.rem(col // 2, 4), lax.rem(col, 2)
    sib = 1 - c

    def r4(v):
        return lax.rem(v, 4)

    def dev(x_=x, zl_=zl, y_=y, zh_=zh, c_=c):
        return (x_ * 4 + zl_, y_ * 8 + zh_ * 2 + c_)

    def at(axis, k):
        here = {"x": x, "zl": zl, "y": y, "zh": zh}[axis]
        there = r4(here + k)
        return dev(**{axis + "_": there}), there

    def send(src, dst, key, device, group=0):
        pltpu.make_async_remote_copy(
            src_ref=src, dst_ref=dst, send_sem=ss.at[group], recv_sem=rs.at[of(*key)],
            device_id=device, device_id_type=MESH,
        ).start()

    def arrive(ref, key):
        pltpu.make_async_remote_copy(
            src_ref=ref, dst_ref=ref, send_sem=ss.at[0], recv_sem=rs.at[of(*key)],
            device_id=dev(c_=sib), device_id_type=MESH,
        ).wait_recv()

    def sent(ref, group):
        pltpu.make_async_remote_copy(
            src_ref=ref, dst_ref=ref, send_sem=ss.at[group], recv_sem=rs.at[0],
            device_id=dev(c_=sib), device_id_type=MESH,
        ).wait_send()

    loads = [
        pltpu.make_async_copy(src, dst, ins.at[n])
        for n, (src, dst) in enumerate(
            [
                (feat_h, fa.at[row]), (cot_h, ca.at[col]), (weight_h, weight),
                (vals_h, vals), (idx_h, idxs),
            ]
        )
    ]
    for load in loads:
        load.start()

    barrier = pltpu.get_barrier_semaphore()
    x_peers, zl_peers, y_peers = ([at(a, k)[0] for k in (1, 2, 3)] for a in ("x", "zl", "y"))
    zh_peers = [at("zh", k)[0] for k in (1, 3)]
    partners = [*x_peers, *zl_peers, *y_peers, *zh_peers, dev(c_=sib)]
    for p in partners:
        pl.semaphore_signal(barrier, inc=1, device_id=p, device_id_type=MESH)

    loads[0].wait()
    loads[1].wait()
    pl.semaphore_wait(barrier, len(partners))

    def tell(n, devices):
        for p in devices:
            pl.semaphore_signal(near.at[n], inc=1, device_id=p, device_id_type=MESH)

    tell(0, zh_peers)
    tell(2, x_peers)
    shifts = [(a, b) for a in (1, 3, 2, 0) for b in (1, 3, 2, 0) if a or b]

    def features_on(block, tag):
        for k in (1, 2, 3):
            d, _ = at("x", k)
            send(fa.at[block], fa.at[block], ("fx", tag), d)

    def cotangents_on(block, tag):
        for k in (1, 2, 3):
            d, _ = at("y", k)
            send(ca.at[block], ca.at[block], ("cy", tag), d)
        send(ca.at[block], ca.at[block], ("cs",), dev(c_=sib))

    for k in (1, 3):
        send(ca.at[col], ca.at[col], ("cz", k), at("zh", k)[0])
    for k in (1, 3):
        send(fa.at[row], fa.at[row], ("fz", k), at("zl", k)[0])
    cotangents_on(col, 0)
    features_on(row, 0)

    for load in loads[2:]:
        load.wait()
    lane = lax.broadcasted_iota(jnp.int32, (1, 128), 1)
    count = cnt[0, 0]
    none = jnp.full((1, 128), 32, jnp.int32)
    zero = jnp.zeros((1, 128), jnp.int32)

    def place(t, carry):
        srow, scol = carry
        i = idxs[0, t]
        here = lane == t
        return jnp.where(here, i // 16, srow), jnp.where(here, lax.rem(i, 16), scol)

    srow, scol = lax.fori_loop(0, 32, place, (zero, zero))

    def link(t, carry):
        pf, lf, pb, lb = carry
        i = idxs[0, t]
        ti, tj = i // 16, lax.rem(i, 16)
        later = lane > t
        pf = jnp.where(later & (srow == ti), t, pf)
        pb = jnp.where(later & (scol == tj), t, pb)
        live = jnp.full((1, 128), t, jnp.int32) < count
        lf = jnp.where(live & (lane == ti), t, lf)
        lb = jnp.where(live & (lane == tj), t, lb)
        return pf, lf, pb, lb

    pf, lf, pb, lb = lax.fori_loop(0, 32, link, (none, none, none, none))
    for n, line in enumerate((scol, pf, lf, srow, pb, lb)):
        tbl_v[n : n + 1, :] = line
    table = pltpu.make_async_copy(tbl_v, tbl_s, ls)
    table.start()
    run[32] = jnp.zeros_like(run[32])

    def turn(s, carry):
        vals_t[s] = vals[s].T
        return carry

    def project(block):
        proj[block] = jnp.dot(fa[block], weight[...], preferred_element_type=F32).astype(BF)
        fa_t[block] = fa[block].T

    lax.fori_loop(0, 32, turn, 0, unroll=4)

    def features_in(k):
        block = x * 4 + r4(zl + 4 - k)
        arrive(fa.at[block], ("fz", k))
        features_on(block, k)

    far = y * 8 + r4(zh + 2) * 2 + c
    halves = (pl.ds(0, 64), pl.ds(64, 64))
    for n, k in enumerate((1, 3)):
        block = y * 8 + r4(zh + 4 - k) * 2 + c
        arrive(ca.at[block], ("cz", k))
        half = ca.at[block, halves[n]]
        send(half, half, ("ch",), at("zh", k)[0])
        cotangents_on(block, k)

    def across(tag):
        arrive(ca.at[pl.ds(0, 3)], ("cy", tag))
        for k in (1, 3, 2):
            block = r4(y + 4 - k) * 8 + r4(zh + 4 - tag) * 2 + c
            send(ca.at[block], ca.at[block], ("cs",), dev(c_=sib))

    send(fa.at[row], fa.at[row], ("fz", 2), at("zl", 2)[0])
    pl.semaphore_wait(near.at[0], 2)
    tell(1, zl_peers)
    across(0)
    for k in (1, 3, 2):
        features_in(k)
    for k in (0, 1, 3, 2):
        project(x * 4 + r4(zl + 4 - k))
    arrive(ca.at[far], ("ch",))
    cotangents_on(far, 2)
    across(1)
    across(3)
    for tag in (0, 1, 3, 2):
        arrive(fa.at[pl.ds(0, 3)], ("fx", tag))
        for k in (1, 3, 2):
            project(r4(x + 4 - k) * 4 + r4(zl + 4 - tag))
    table.wait()

    def chain(left, right, at_line, previous_line):
        def some(q, carry):
            products = [
                jnp.dot(left[q * 8 + u], right[tbl_s[at_line, q * 8 + u]], preferred_element_type=F32)
                for u in range(8)
            ]
            for u in range(8):
                run[q * 8 + u] = products[u] + run[tbl_s[previous_line, q * 8 + u]]
            return carry

        lax.fori_loop(0, 4, some, 0)

    chain(vals, proj, 0, 1)

    def forward_out(o, carry):
        r = lax.rem(o, 4) * 8 + lax.rem(o // 4, 4) * 2 + o // 16
        pout[o] = run[tbl_s[2, r]].astype(BF)
        return carry

    lax.fori_loop(0, 32, forward_out, 0)

    def group(g):
        return r4(zh + ORDER[g])

    def out_y(g):
        arrive(rc.at[pl.ds(g * 4, 4)], ("oc", g))
        for k in (2, 1, 3):
            d, there = at("y", k)
            own = pout[c * 16 + group(g) * 4 + there].astype(F32)
            sy[g * 3 + k - 1] = (own + rc[g * 4 + there].astype(F32)).astype(BF)
            send(sy.at[g * 3 + k - 1], ry.at[g * 3 + k - 1], ("oy", g), d, 1)
        own_y[g] = pout[c * 16 + group(g) * 4 + y].astype(F32) + rc[g * 4 + y].astype(F32)

    across(2)
    for g in range(4):
        part = pl.ds(sib * 16 + group(g) * 4, 4)
        send(pout.at[part], rc.at[pl.ds(g * 4, 4)], ("oc", g), dev(c_=sib), 1)
    out_y(0)

    def total_y(g):
        total = own_y[g]
        arrive(ry.at[pl.ds(g * 3, 3)], ("oy", g))
        for k in (1, 2, 3):
            total = total + ry[g * 3 + k - 1].astype(F32)
        return total

    def out_z(g):
        sz[g] = total_y(g).astype(BF)
        if g == 0:
            for n, k in enumerate((1, 3)):
                send(sz.at[0, halves[n]], relay.at[n], ("or", n), at("zh", k)[0], 1)
            return
        n = g - 1
        arrive(relay.at[n], ("or", n))
        sz[g, halves[n], :] = (sz[g, halves[n], :].astype(F32) + relay[n].astype(F32)).astype(BF)
        send(sz.at[g], rz.at[n], ("oz",), at("zh", ORDER[g])[0], 1)

    def out_end():
        total = total_y(3)
        arrive(rz, ("oz",))
        for n in range(2):
            total = total + rz[n].astype(F32)
        out_o[...] = total.astype(BF)

    arrive(ca.at[pl.ds(0, 16)], ("cs",))

    chain(vals_t, ca, 3, 4)

    def backward_out(j, carry):
        pback[j] = run[tbl_s[5, j]].astype(BF)
        return carry

    lax.fori_loop(0, 16, backward_out, 0)

    term = jnp.zeros((256, 256), F32)
    for j in range(16):
        term += jnp.dot(fa_t[j], pback[j], preferred_element_type=F32)
    wacc[...] = term
    wb[...] = term.astype(BF)
    send(wb.at[pl.ds(pl.multiple_of(sib * 128, 128), 128)], w0r, ("w0",), dev(c_=sib), 2)

    def term_xy():
        arrive(w0r, ("w0",))
        half = wacc[pl.ds(pl.multiple_of(c * 128, 128), 128), :] + w0r[...].astype(F32)
        for p in range(16):
            piece = half[p // 2 * 16 : p // 2 * 16 + 16, p % 2 * 128 : p % 2 * 128 + 128]
            wh[p] = piece
            w1s[p] = piece.astype(BF)
        pl.semaphore_wait(near.at[2], 3)
        for kx, ky in shifts:
            there_x, there_y = r4(x + kx), r4(y + ky)
            send(
                w1s.at[there_x * 4 + there_y], w1r.at[kx * 4 + ky - 1], ("w1",),
                dev(x_=there_x, y_=there_y), 3,
            )

    def term_z():
        arrive(w1r, ("w1",))
        small = wh[x * 4 + y]
        for n in range(15):
            small = small + w1r[n].astype(F32)
        mine = w3.at[zl * 4 + zh]
        mine[...] = small.astype(BF)
        pl.semaphore_wait(near.at[1], 3)
        for kl, kh in shifts:
            send(mine, mine, ("w3",), dev(zl_=r4(zl + kl), zh_=r4(zh + kh)), 4)

    def back_xy():
        arrive(w3.at[pl.ds(0, 15)], ("w3",))
        total = w3[0].astype(F32)
        for n in range(1, 16):
            total = total + w3[n].astype(F32)
        mine = w6.at[x * 4 + y]
        mine[...] = (total * (1.0 / math.sqrt(65536))).astype(BF)
        for kx, ky in shifts:
            send(mine, mine, ("w6",), dev(x_=r4(x + kx), y_=r4(y + ky)), 5)

    def back_core():
        arrive(w6.at[pl.ds(0, 15)], ("w6",))
        send(w6, w8r, ("w8",), dev(c_=sib), 2)

    def back_end():
        for here, ref in ((c, w6), (sib, w8r)):
            if ref is w8r:
                arrive(w8r, ("w8",))
            for p in range(16):
                at_row = pl.multiple_of(here * 128 + p // 2 * 16, 16)
                wg_o[pl.ds(at_row, 16), p % 2 * 128 : p % 2 * 128 + 128] = ref[p].astype(F32)

    def grad_x(g):
        zt = r4(zl + ORDER[g])
        for k in (2, 1, 3):
            d, there = at("x", k)
            send(pback.at[there * 4 + zt], rx.at[g * 3 + k - 1], ("bx", g), d, 1)

    def total_x(g):
        total = pback[x * 4 + r4(zl + ORDER[g])].astype(F32)
        arrive(rx.at[pl.ds(g * 3, 3)], ("bx", g))
        for k in (1, 2, 3):
            total = total + rx[g * 3 + k - 1].astype(F32)
        return total

    def grad_z(g):
        szl[g] = total_x(g).astype(BF)
        send(szl.at[g], rzl.at[g], ("bz",), at("zl", ORDER[g])[0], 1)

    def grad_end():
        grad = total_x(3)
        arrive(rzl, ("bz",))
        for g in range(3):
            grad = grad + rzl[g].astype(F32)
        high = grad.astype(BF)
        low = (grad - high.astype(F32)).astype(BF)
        nt = (((1,), (1,)), ((), ()))
        ig_o[...] = (
            lax.dot_general(high, weight[...], nt, preferred_element_type=F32)
            + lax.dot_general(low, weight[...], nt, preferred_element_type=F32)
        ).astype(BF)

    term_xy()
    tell(4, [dev(c_=sib)])
    pl.semaphore_wait(near.at[4], 1)
    out_y(1)
    out_y(2)
    grad_x(0)
    out_z(0)
    term_z()
    tell(3, [dev(c_=sib)])
    pl.semaphore_wait(near.at[3], 1)
    out_z(1)
    out_y(3)
    grad_x(1)
    grad_x(2)
    grad_x(3)
    out_z(2)
    back_xy()
    grad_z(0)
    grad_z(1)
    grad_z(2)
    out_end()
    back_core()
    grad_end()
    back_end()

    for group, ref in enumerate((run.at[pl.ds(0, 23)], run.at[pl.ds(0, 23)], fa.at[pl.ds(0, 2)], w1r, w1r, w1r)):
        sent(ref, group)


def hand_over(*refs):
    copies = [pltpu.make_async_copy(refs[n], refs[n + 3], refs[6].at[n]) for n in range(3)]
    for copy in copies:
        copy.start()
    for copy in copies:
        copy.wait()


def body(features, weight, cotangent, block_index, block_count, block_values):
    hbm = pl.BlockSpec(memory_space=pltpu.HBM)
    index = block_index.reshape(1, 32)
    operands = [
        pltpu.with_memory_space_constraint(a, pltpu.HBM)
        for a in (features, weight, cotangent, block_values.reshape(32, 128, 128), index)
    ]
    blocks = functools.partial(lambda dtype, n: pltpu.VMEM((n, 128, 256), dtype))
    shapes = (
        jax.ShapeDtypeStruct((128, 256), BF),
        jax.ShapeDtypeStruct((128, 256), BF),
        jax.ShapeDtypeStruct((256, 256), F32),
    )
    vmem = pl.BlockSpec(memory_space=pltpu.VMEM)
    results = pl.pallas_call(
        kernel,
        out_shape=shapes,
        in_specs=[hbm] * 5 + [pl.BlockSpec(memory_space=pltpu.SMEM)],
        out_specs=(vmem, vmem, vmem),
        scratch_shapes=[
            pltpu.VMEM((256, 256), BF), pltpu.VMEM((32, 128, 128), BF), pltpu.VMEM((32, 128, 128), BF),
            blocks(BF, 16), pltpu.VMEM((16, 256, 128), BF), blocks(BF, 32), blocks(BF, 16), blocks(F32, 33),
            blocks(BF, 32), blocks(BF, 16),
            pltpu.VMEM((8, 128), jnp.int32), pltpu.SMEM((8, 128), jnp.int32),
            blocks(BF, 16), blocks(BF, 12), blocks(F32, 4), blocks(BF, 12),
            blocks(BF, 3), blocks(BF, 2), pltpu.VMEM((2, 64, 256), BF), blocks(BF, 12), blocks(BF, 3), blocks(BF, 3),
            pltpu.VMEM((256, 256), F32), pltpu.VMEM((256, 256), BF), pltpu.VMEM((128, 256), BF),
            pltpu.VMEM((16, 16, 128), F32), *(pltpu.VMEM((n, 16, 128), BF) for n in (16, 15, 16, 16, 16)),
            pltpu.SMEM((1, 32), jnp.int32),
            pltpu.SemaphoreType.DMA((6,)), pltpu.SemaphoreType.DMA((KEYS,)),
            pltpu.SemaphoreType.DMA, pltpu.SemaphoreType.DMA((5,)), pltpu.SemaphoreType.REGULAR((5,)),
        ],
        compiler_params=pltpu.CompilerParams(
            collective_id=0, has_side_effects=True, vmem_limit_bytes=48 << 20
        ),
        name="graph_step",
    )(*operands, block_count)
    return pl.pallas_call(
        hand_over,
        out_shape=shapes,
        in_specs=[vmem] * 3,
        out_specs=(hbm, hbm, hbm),
        scratch_shapes=[pltpu.SemaphoreType.DMA((3,))],
        name="hand_over",
    )(*(pltpu.with_memory_space_constraint(r, pltpu.VMEM) for r in results))


def solution(mesh):
    in_specs = (
        P(("col", "row"), None),
        P(),
        P(("row", "col"), None),
        P("row", "col", None),
        P("row", "col"),
        P("row", "col", None, None, None),
    )
    out_specs = (P(("row", "col"), None), P(("col", "row"), None), P())
    return jax.shard_map(body, mesh=mesh, in_specs=in_specs, out_specs=out_specs, check_vma=False)
```
